256 devices in a mesh: store: 8 (over y, core), tensor: 32 (over z, x).
Axes of the slice: x: 4, y: 4, z: 8, core: 2. Of those that a mesh axis runs over, the one named last changes fastest.
Arguments:
- decoder_rows: bfloat16 [16384, 4096], P(('store', 'tensor')), may hold values from -45 to 45
- q_weight: bfloat16 [4096, 4096], P(None, 'tensor'), may hold values from -0.09375 to 0.09375
- kv_weight: bfloat16 [2, 896, 4096], P(None, None, 'tensor'), may hold values from -0.1875 to 0.1875
- out_weight: bfloat16 [4096, 4096], P('tensor'), may hold values from -0.5 to 0.5
- store_tiles: bfloat16 [4096, 128, 896], P('store', 'tensor'), may hold values from -6 to 6
- neighbour_shard: int32 [256, 2], replicated, may hold values from 0 to 7, all different within a row; in each aligned block of 32 rows (0 to 31, 32 to 63, ...) at most 12 rows name the same one
- neighbour_tile: int32 [256, 2], replicated, may hold values from 0 to 511
Outputs:
- cross: bfloat16 [16384, 4096], P(('store', 'tensor'))
The draws below stay inside these ranges and needn't reach their ends.
Inputs may be any that keep to these rules, and one draw needn't show every extreme that they name: `neighbour_shard`: each block's 2 neighbours lie in different shards; among the 32 blocks of one sequence no shard is named more than 12 times, and in some sequence one shard is named exactly 12 times.
All inputs are finite; a program needn't handle non-finite values.
Results may differ from the reference program's by a relative error of at most 0.023.
Values may be sent and summed in bfloat16 or wider, within the bound.
No kernel may reach another device: no remote copies, remote signals or barrier semaphores. Data moves between devices by JAX's collectives and lax.ppermute only.
A program may use at most 128 MiB of HBM per device.

```python
import math
import jax
import jax.numpy as jnp
import numpy as np
from jax import lax

D = 4096
HEADS = 32
HD = 128
ENC = 896
BLOCK = 64
NTOK = 128
NEIGH = 2
TOK_DEV = 64
TILES_SH = 512
CG = 32
SPANS = 256
TOKENS = 16384
CAP = 12
TILES = 4096
N_STORE = 8
N_TENSOR = 32


def draw_decoder_rows(key, part):
    key_rows, key_cols, key_base = jax.random.split(key, 3)
    row_factor = jnp.exp(jax.random.uniform(key_rows, (TOKENS, 1), jnp.float32, math.log(0.3), math.log(3.0)))
    col_factor = jnp.exp(jax.random.uniform(key_cols, (1, D), jnp.float32, math.log(0.3), math.log(3.0)))
    base_value = jnp.clip(jax.random.normal(key_base, (TOKENS, D), jnp.float32), -5.0, 5.0)
    return (base_value * row_factor * col_factor).astype(jnp.bfloat16)


def set_ends(values, stream_key, smallest, top_value):
    dims = values.shape
    place = [jax.random.randint(jax.random.fold_in(stream_key, axis), (), 0, dims[axis]) for axis in range(len(dims))]
    values = values.at[tuple(place)].set(smallest)
    longest = dims.index(max(dims))
    place[longest] = (place[longest] + 1) % dims[longest]
    return values.at[tuple(place)].set(top_value)


def levels(stream_key, shape, cuts, least, largest):
    loudness, own = 1.0, jax.random.fold_in(stream_key, 6)
    for dim, blocks in cuts:
        heights = jnp.exp(jax.random.uniform(jax.random.fold_in(own, dim), (blocks,), jnp.float32, least / len(cuts), largest / len(cuts)))
        loudness = loudness * jnp.repeat(heights, shape[dim] // blocks).reshape([-1 if axis == dim else 1 for axis in range(len(shape))])
    return loudness


def shared_out(key, own, number, rows, amount, top, most, slope):
    order = jax.random.permutation(key, amount)
    crowded, usual = load_shares(amount, rows * top, most, slope, True), load_shares(amount, rows * top, most, slope, False)
    places = jnp.arange(amount)

    def named(tallies, rotation):
        used = int((tallies > 0).sum())
        fixed = max(1, used // 4)
        moved = fixed + (places - fixed + rotation * (used - fixed)) % max(1, amount - fixed)
        return jnp.zeros((amount,), jnp.int32).at[order[jnp.where(places < fixed, places, moved)]].set(jnp.asarray(tallies, jnp.int32))

    tallies = jnp.where(number % 4 == 0, named(crowded, number // 4), named(usual, number - number // 4 - 1))
    mixed = jax.random.permutation(jax.random.fold_in(own, 3), amount)
    giver, sink = mixed[0:amount // 2 * 2:2], mixed[1:amount // 2 * 2:2]
    room = jnp.minimum(tallies[giver] - 1, most - tallies[sink]) // 2
    room = jnp.where((giver == order[0]) | (sink == order[0]) | (tallies[sink] == 0), 0, jnp.maximum(room, 0))
    moved = jax.random.randint(jax.random.fold_in(own, 4), (amount // 2,), 0, 1 << 20) % (room + 1)
    tallies = tallies.at[giver].add(-moved).at[sink].add(moved)
    items = jnp.searchsorted(jnp.cumsum(tallies), jnp.arange(rows * top), side="right").astype(jnp.int32)
    listing = items.reshape(top, rows).T
    listing = listing[jax.random.permutation(jax.random.fold_in(own, 1), rows)]
    rotation = jax.random.randint(jax.random.fold_in(own, 2), (rows, 1), 0, top)
    return jnp.take_along_axis(listing, (jnp.arange(top)[None, :] + rotation) % top, axis=1)


def load_shares(count, total, reach, skew, full):
    weights = [(1 << 20) // math.isqrt(rank ** skew) + 1 for rank in range(1, count + 1)]
    largest = reach if full else min(reach, max(-(-total // count), total * weights[0] // sum(weights)))
    least = 1 if total - largest >= count - 1 else 0
    given, spare = [largest] + [least] * (count - 1), total - largest - least * (count - 1)
    while spare > 0:
        free = [i for i in range(1, count) if given[i] < largest] or [i for i in range(1, count) if given[i] < reach]
        mass, budget = sum([weights[i] for i in free]), spare
        for i in free:
            more = min(reach - given[i], max(1, budget * weights[i] // mass), spare)
            given[i] = given[i] + more
            spare = spare - more
    return np.array(given)


def noise(own_key, dims, scale, bound, shards=(), kind=jnp.bfloat16):
    factor_of = levels(own_key, dims, shards, -0.22, 0.18) if shards else 1.0
    values = jax.random.normal(own_key, dims, jnp.float32) * scale * factor_of
    return jnp.minimum(jnp.maximum(values, -bound), bound).astype(kind)


def setup_inputs(seed: int = 0) -> dict:
    seeds = jax.random.split(jax.random.key(seed), 8)
    decoder_rows = draw_decoder_rows(jax.random.fold_in(seeds[7], 71), 0)
    q_weight = noise(seeds[1], (D, HEADS * HD), D ** -0.5, 0.09375, ((1, 32),))
    kv_weight = noise(seeds[2], (2, ENC, HEADS * HD), ENC ** -0.5, 0.1875, ((2, 32),))
    out_weight = noise(seeds[3], (HEADS * HD, D), HD ** -0.5, 0.5, ((0, 32),))
    store_tiles = noise(seeds[4], (TILES, NTOK, ENC), 1.0, 6.0, ((0, 8), (1, 32)))
    neighbour_shard_keys = jax.random.split(jax.random.fold_in(seeds[5], 1), SPANS // CG)
    neighbour_shard_turns = jax.random.permutation(jax.random.fold_in(seeds[5], 3), SPANS // CG)
    neighbour_shard = jax.vmap(lambda own, number: shared_out(jax.random.fold_in(seeds[5], 2), own, number, CG, N_STORE, NEIGH, CAP, 2))(neighbour_shard_keys, neighbour_shard_turns).reshape((SPANS, NEIGH))
    neighbour_tile = set_ends(jax.random.randint(seeds[6], (SPANS, NEIGH), 0, TILES_SH), jax.random.fold_in(seeds[6], 1), 0, TILES_SH - 1).astype(jnp.int32)
    return {"decoder_rows": decoder_rows, "q_weight": q_weight, "kv_weight": kv_weight, "out_weight": out_weight, "store_tiles": store_tiles, "neighbour_shard": neighbour_shard, "neighbour_tile": neighbour_tile}


def reference(decoder_rows, q_weight, kv_weight, out_weight, store_tiles, neighbour_shard, neighbour_tile):
    seq_len = TOK_DEV * N_TENSOR
    head_dev = HEADS // N_TENSOR
    q_factor = 1.0 / math.sqrt(HD)
    grouped_rows = decoder_rows.reshape(N_STORE, seq_len, D)
    grouped_shard = neighbour_shard.reshape(N_STORE, CG, NEIGH)
    grouped_tile = neighbour_tile.reshape(N_STORE, CG, NEIGH)
    part_weight = out_weight.reshape(N_TENSOR, head_dev * HD, D)

    def one_sequence(inputs):
        seq_rows, seq_shard, seq_tile = inputs
        rows_wide = seq_rows.astype(jnp.float32)
        normed = (rows_wide * lax.rsqrt(lax.optimization_barrier(jnp.mean(rows_wide * rows_wide, axis=1, keepdims=True)) + 1e-05)).astype(jnp.bfloat16)
        queries = (jnp.dot(normed, q_weight, preferred_element_type=jnp.float32) * q_factor).astype(jnp.bfloat16)
        flat_index = (seq_shard * TILES_SH + seq_tile).reshape(-1).astype(jnp.int32)
        neighbours = jnp.take(store_tiles, flat_index, axis=0)
        keys_values = jnp.einsum('rne,ced->rncd', neighbours.astype(jnp.float32), kv_weight.astype(jnp.float32)).astype(jnp.bfloat16)
        keys_values = lax.optimization_barrier(keys_values)
        keyed = keys_values.reshape(CG, NEIGH * NTOK, 2, HEADS, HD).astype(jnp.float32)
        query_blocks = queries.reshape(CG, BLOCK, HEADS, HD).astype(jnp.float32)
        scores = jnp.einsum('cqhd,ckhd->chqk', query_blocks, keyed[:, :, 0])
        expo_scores = jnp.exp(scores)
        weights = (expo_scores / lax.optimization_barrier(jnp.sum(expo_scores, axis=3, keepdims=True))).astype(jnp.bfloat16)
        weights = lax.optimization_barrier(weights).astype(jnp.float32)
        attended = jnp.einsum('chqk,ckhd->cqhd', weights, keyed[:, :, 1]).astype(jnp.bfloat16)
        part_rows = attended.reshape(seq_len, N_TENSOR, head_dev * HD)

        def add_partial(head_group, running):
            rows_part = lax.dynamic_index_in_dim(part_rows, head_group, 1, keepdims=False)
            weight_part = lax.dynamic_index_in_dim(part_weight, head_group, 0, keepdims=False)
            partial_term = jnp.dot(rows_part, weight_part, preferred_element_type=jnp.float32).astype(jnp.bfloat16)
            partial_term = lax.optimization_barrier(partial_term)
            return running + partial_term.astype(jnp.float32)
        summed = lax.fori_loop(0, N_TENSOR, add_partial, jnp.zeros((seq_len, D), jnp.float32))
        return summed.astype(jnp.bfloat16)
    result = lax.map(one_sequence, (grouped_rows, grouped_shard, grouped_tile))
    return result.reshape(TOKENS, D)
```

```python
import functools
import math

import jax
import jax.numpy as jnp
from jax import lax
from jax.experimental import pallas as pl
from jax.experimental.pallas import tpu as pltpu
from jax.sharding import Mesh, PartitionSpec as P

HD = 128
BLOCK = 64
NTOK = 128
NEIGH = 2
Y, C, Z, X = 4, 2, 8, 4
ROW_AXES = ("c", "x")
GROUP = C * X
HEADS_HERE = 4
ENC = 896
D = 4096


def ring_pairs():
    up = [(z, (z + 1) % Z) for z in range(Z)]
    down = [(Z + z, Z + (z - 1) % Z) for z in range(Z)]
    return up + down


def first_pairs():
    keep = [(z, z) for z in range(Z)]
    down = [(Z + z, Z + (z - 1) % Z) for z in range(Z)]
    return keep + down


def ring(own):
    held = lax.ppermute(own, ("c", "z"), first_pairs())
    pieces = [held]
    for _ in range(HEADS_HERE - 1):
        held = lax.ppermute(held, ("c", "z"), ring_pairs())
        pieces.append(held)
    return pieces


def attend_kernel(q0, q1, q2, q3, nb, k0, k1, k2, k3, o0, o1, o2, o3, out, wkv, wo):
    @pl.when(pl.program_id(0) == 0)
    def _():
        for h, (kv_h, o_h) in enumerate(((k0, o0), (k1, o1), (k2, o2), (k3, o3))):
            wkv[:, h * HD : (h + 1) * HD] = kv_h[0]
            wkv[:, (HEADS_HERE + h) * HD : (HEADS_HERE + h + 1) * HD] = kv_h[1]
            wo[h * HD : (h + 1) * HD, :] = o_h[...]

    tokens = nb[...].reshape(NEIGH * NTOK, ENC)
    keys_values = jnp.dot(tokens, wkv[...], preferred_element_type=jnp.float32).astype(
        jnp.bfloat16
    )
    parts = []
    for h, q_h in enumerate((q0, q1, q2, q3)):
        keys = keys_values[:, h * HD : (h + 1) * HD]
        values = keys_values[:, (HEADS_HERE + h) * HD : (HEADS_HERE + h + 1) * HD]
        scores = lax.dot_general(
            q_h[...], keys, (((1,), (1,)), ((), ())), preferred_element_type=jnp.float32
        )
        expo = jnp.exp(scores)
        weights = (expo / jnp.sum(expo, axis=1, keepdims=True)).astype(jnp.bfloat16)
        parts.append(
            jnp.dot(weights, values, preferred_element_type=jnp.float32).astype(jnp.bfloat16)
        )
    attended = jnp.concatenate(parts, axis=1)
    for n in range(0, D, 512):
        out[:, n : n + 512] = jnp.dot(
            attended, wo[:, n : n + 512], preferred_element_type=jnp.float32
        ).astype(jnp.bfloat16)


def attend(queries, neighbours, kvs, outs):
    const2 = lambda g: (0, 0)
    const3 = lambda g: (0, 0, 0)
    return pl.pallas_call(
        attend_kernel,
        grid=(GROUP,),
        in_specs=[pl.BlockSpec((BLOCK, HD), lambda g: (g, 0))] * 4
        + [
            pl.BlockSpec(
                (None, X, None, NEIGH, NTOK // X, ENC),
                lambda g: (g // X, 0, g % X, 0, 0, 0),
            )
        ]
        + [pl.BlockSpec((2, ENC, HD), const3)] * 4
        + [pl.BlockSpec((HD, D), const2)] * 4,
        out_specs=pl.BlockSpec((BLOCK, D), lambda g: (g, 0)),
        out_shape=jax.ShapeDtypeStruct((GROUP * BLOCK, D), jnp.bfloat16),
        scratch_shapes=[
            pltpu.VMEM((ENC, 2 * HEADS_HERE * HD), jnp.bfloat16),
            pltpu.VMEM((HEADS_HERE * HD, D), jnp.bfloat16),
        ],
        compiler_params=pltpu.CompilerParams(vmem_limit_bytes=48 << 20),
        cost_estimate=pl.CostEstimate(
            flops=7_000_000_000, bytes_accessed=16_000_000, transcendentals=524_288
        ),
    )(*queries, neighbours, *kvs, *outs)


def body(
    decoder_rows, q_weight, kv_weight, out_weight, store_tiles, neighbour_shard, neighbour_tile
):
    store_count = Y * C
    my_sequence = lax.axis_index(("y", "c"))
    request_count = Z * X * NEIGH
    capacity = 3 * request_count // (2 * store_count)
    q_factor = 1.0 / math.sqrt(HD)

    rows_wide = decoder_rows.astype(jnp.float32)
    normed = (
        rows_wide * lax.rsqrt(jnp.mean(rows_wide * rows_wide, axis=1, keepdims=True) + 1e-05)
    ).astype(jnp.bfloat16)
    rows = lax.all_gather(normed, ROW_AXES, axis=0, tiled=True)

    q_pieces = ring(q_weight)
    kv_pieces = ring(kv_weight)
    out_pieces = ring(out_weight)

    shard_table = neighbour_shard.reshape(store_count, request_count)
    tile_table = neighbour_tile.reshape(store_count, request_count)
    positions = jnp.arange(request_count, dtype=jnp.int32)
    before_mask = positions[None, :] < positions[:, None]
    same_shard = shard_table[:, :, None] == shard_table[:, None, :]
    rank_table = jnp.sum((same_shard & before_mask[None]).astype(jnp.int32), axis=2)
    served_here = shard_table == my_sequence
    slot_ids = jnp.arange(capacity, dtype=jnp.int32)
    slot_match = (
        served_here[:, :, None] & (rank_table[:, :, None] == slot_ids[None, None, :])
    ).astype(jnp.int32)
    slot_tile = jnp.sum(slot_match * tile_table[:, :, None], axis=1)
    outgoing = jnp.take(store_tiles, slot_tile.reshape(-1), axis=0)
    arrived = lax.all_to_all(outgoing, ("y", "c"), split_axis=0, concat_axis=0, tiled=True)
    own_shard = lax.dynamic_index_in_dim(shard_table, my_sequence, 0, keepdims=False)
    own_rank = lax.dynamic_index_in_dim(rank_table, my_sequence, 0, keepdims=False)
    slot_index = own_shard * capacity + own_rank
    wanted = jnp.take(arrived, slot_index, axis=0)
    slices = lax.all_to_all(wanted, "z", split_axis=0, concat_axis=0, tiled=True)
    per_z = X * NEIGH
    own_tokens = store_tiles.shape[1]
    column = (
        slices.reshape(Z, per_z, own_tokens, ENC)
        .transpose(1, 0, 2, 3)
        .reshape(per_z, Z * own_tokens, ENC)
    )
    neighbours = lax.all_gather(column, ROW_AXES, axis=0, tiled=True).reshape(
        C, X, X, NEIGH, Z * own_tokens, ENC
    )

    queries = [
        (jnp.dot(rows, piece, preferred_element_type=jnp.float32) * q_factor).astype(jnp.bfloat16)
        for piece in q_pieces
    ]
    partial = attend(queries, neighbours, kv_pieces, out_pieces)
    return lax.psum_scatter(partial, ROW_AXES, scatter_dimension=0, tiled=True)


def solution(mesh):
    grid = Mesh(mesh.devices.reshape(Y, C, Z, X), ("y", "c", "z", "x"))
    tensor = ("z", "x")
    store = ("y", "c")
    in_specs = (
        P(("y", "c", "z", "x"), None),
        P(None, tensor),
        P(None, None, tensor),
        P(tensor, None),
        P(store, tensor, None),
        P(),
        P(),
    )
    out_specs = P(("y", "c", "z", "x"), None)
    return jax.shard_map(body, mesh=grid, in_specs=in_specs, out_specs=out_specs, check_vma=False)
```

```python
import functools
import math

import jax
import jax.numpy as jnp
from jax import lax
from jax.experimental import pallas as pl
from jax.experimental.pallas import tpu as pltpu
from jax.sharding import Mesh, PartitionSpec as P

HD = 128
BLOCK = 64
NTOK = 128
NEIGH = 2
Y, C, Z, X = 4, 2, 8, 4
ROW_AXES = ("c", "x")
GROUP = C * X
HEADS_HERE = 4
ENC = 896
D = 4096


def move(value, pairs):
    return lax.ppermute(value, ("c", "z"), [(c * Z + z, d * Z + w % Z) for c, z, d, w in pairs])


def hop(value, by=1):
    return move(
        value,
        [(0, z, 0, z + by) for z in range(Z)] + [(1, z, 1, z - by) for z in range(Z)],
    )


def last_hop(own, third):
    half = own.shape[0] // 2
    low = move(third[:half], [(1, z, 1, z - 1) for z in range(Z)])
    high = move(third[half:], [(0, z, 1, z + 1) for z in range(Z)])
    return jnp.where(lax.axis_index("c") == 0, own, jnp.concatenate([low, high], axis=0))


def shift(value, axis, by):
    size = lax.axis_size(axis)
    return lax.ppermute(value, axis, [(i, (i + by) % size) for i in range(size)])


def tie(value, *others):
    return lax.optimization_barrier((value, *others))[0]


IN_VMEM = pl.BlockSpec(memory_space=pltpu.VMEM)
IN_SMEM = pl.BlockSpec(memory_space=pltpu.SMEM)


OUT_COLS = D // Y
UNPACK_FLOPS = 18_000_000_000


def unpack_kernel(place, *refs):
    *pieces, wo = refs
    for b in range(2):
        own, up, far0, far1, down = pieces[5 * b : 5 * b + 5]
        for k in range(2):
            row = (2 * b + k) * HD
            for step, piece in enumerate((own.at[k], up.at[k], (far0, far1)[k], down.at[k])):
                quarter = lax.rem(place[2] + step, Y)
                column = pl.multiple_of(quarter * OUT_COLS, OUT_COLS)
                wo[row : row + HD, pl.ds(column, OUT_COLS)] = piece[...]


def unpack(place, pieces):
    return pl.pallas_call(
        unpack_kernel,
        in_specs=[IN_SMEM] + [IN_VMEM] * len(pieces),
        out_specs=IN_VMEM,
        out_shape=jax.ShapeDtypeStruct((HEADS_HERE * HD, D), jnp.bfloat16),
        cost_estimate=pl.CostEstimate(
            flops=UNPACK_FLOPS, bytes_accessed=10_000, transcendentals=0
        ),
    )(place, *pieces)


def attend_kernel(place, q0, q1, q2, q3, kv0, kv1, kv2, kv3, nb, attended, wkv):
    for h, kv in enumerate((kv0, kv1, kv2, kv3)):
        for a in range(2):
            column = (2 * h + a) * HD
            wkv[:, column : column + HD] = kv[a]
    my_c = place[0]
    my_x = place[1]
    for j in range(GROUP):
        if j < C:
            core = lax.rem(my_c + 1 + j, C)
            block = lax.rem(my_x + 2, X)
        else:
            core = lax.rem(my_c + (1 if j < C + X - 1 else 0), C)
            block = lax.rem(my_x + 3 + (j - C) % (X - 1), X)
        tokens = nb[core, :, block].reshape(NEIGH * NTOK, ENC)
        keys_values = jnp.dot(tokens, wkv[...], preferred_element_type=jnp.float32).astype(
            jnp.bfloat16
        )
        first = pl.multiple_of((core * X + block) * BLOCK, BLOCK)
        for h, q_h in enumerate((q0, q1, q2, q3)):
            keys = keys_values[:, 2 * h * HD : (2 * h + 1) * HD]
            values = keys_values[:, (2 * h + 1) * HD : (2 * h + 2) * HD]
            scores = lax.dot_general(
                q_h[pl.ds(first, BLOCK), :],
                keys,
                (((1,), (1,)), ((), ())),
                preferred_element_type=jnp.float32,
            )
            expo = jnp.exp(scores)
            weights = (expo / jnp.sum(expo, axis=1, keepdims=True)).astype(jnp.bfloat16)
            attended[j * BLOCK : (j + 1) * BLOCK, h * HD : (h + 1) * HD] = jnp.dot(
                weights, values, preferred_element_type=jnp.float32
            ).astype(jnp.bfloat16)


def attend(place, queries, kvs, neighbours):
    return pl.pallas_call(
        attend_kernel,
        in_specs=[IN_SMEM] + [IN_VMEM] * (2 * HEADS_HERE + 1),
        out_specs=IN_VMEM,
        out_shape=jax.ShapeDtypeStruct((GROUP * BLOCK, HEADS_HERE * HD), jnp.bfloat16),
        scratch_shapes=[pltpu.VMEM((ENC, 2 * HEADS_HERE * HD), jnp.bfloat16)],
        compiler_params=pltpu.CompilerParams(vmem_limit_bytes=24 << 20),
        cost_estimate=pl.CostEstimate(
            flops=1_000_000, bytes_accessed=10_000, transcendentals=0
        ),
    )(place, *queries, *kvs, neighbours)


def add(*terms):
    return sum(t.astype(jnp.float32) for t in terms).astype(jnp.bfloat16)


def project_and_reduce(attended, wo):
    half = D // 2
    far_end = C * BLOCK
    other_end = far_end + (X - 1) * BLOCK

    def project(first, last):
        rows = jnp.dot(attended[first:last], wo, preferred_element_type=jnp.float32)
        return rows.astype(jnp.bfloat16).reshape(-1, BLOCK, D)

    far = project(0, far_end)
    far_swapped = shift(far[0], "c", 1)
    for_other = project(far_end, other_end)
    swapped = shift(for_other, "c", 1)
    far_sum = add(far[1], far_swapped)
    far_up = shift(far_sum[:, :half], "x", 1)
    far_down = shift(far_sum[:, half:], "x", -1)
    own = project(other_end, GROUP * BLOCK)
    empty = jnp.zeros((BLOCK, half), jnp.bfloat16)
    up_sum = add(own[2], swapped[2], jnp.concatenate([far_up, empty], axis=1))
    down_sum = add(own[0], swapped[0], jnp.concatenate([empty, far_down], axis=1))
    from_below = shift(up_sum, "x", 1)
    from_above = shift(down_sum, "x", -1)
    return add(own[1], swapped[1], from_below, from_above)


def project_queries(rows, weight):
    q_factor = 1.0 / math.sqrt(HD)
    wide = jnp.dot(rows, weight, preferred_element_type=jnp.float32)
    return (wide * q_factor).astype(jnp.bfloat16)


def body(
    decoder_rows, q_weight, kv_weight, out_weight, store_tiles, neighbour_shard, neighbour_tile
):
    store_count = Y * C
    my_sequence = lax.axis_index(("y", "c"))
    request_count = Z * X * NEIGH
    capacity = 3 * request_count // (2 * store_count)

    rows_wide = decoder_rows.astype(jnp.float32)
    normed = (
        rows_wide * lax.rsqrt(jnp.mean(rows_wide * rows_wide, axis=1, keepdims=True) + 1e-05)
    ).astype(jnp.bfloat16)
    rows = lax.all_gather(normed, ROW_AXES, axis=0, tiled=True)

    place = jnp.stack([lax.axis_index(axis) for axis in ("c", "x", "y")]).astype(jnp.int32)
    q_hops = [hop(q_weight)]
    kv_hops = [hop(kv_weight)]
    out_own = lax.dynamic_slice_in_dim(out_weight, place[2] * OUT_COLS, OUT_COLS, axis=1)
    out_near = [hop(out_own), hop(out_own, 2)]

    shard_table = neighbour_shard.reshape(store_count, request_count)
    tile_table = neighbour_tile.reshape(store_count, request_count)
    positions = jnp.arange(request_count, dtype=jnp.int32)
    before_mask = positions[None, :] < positions[:, None]
    same_shard = shard_table[:, :, None] == shard_table[:, None, :]
    rank_table = jnp.sum((same_shard & before_mask[None]).astype(jnp.int32), axis=2)
    served_here = shard_table == my_sequence
    slot_ids = jnp.arange(capacity, dtype=jnp.int32)
    slot_match = (
        served_here[:, :, None] & (rank_table[:, :, None] == slot_ids[None, None, :])
    ).astype(jnp.int32)
    slot_tile = jnp.sum(slot_match * tile_table[:, :, None], axis=1)
    outgoing = jnp.take(store_tiles, slot_tile.reshape(-1), axis=0, mode="clip")
    arrived = lax.all_to_all(outgoing, ("y", "c"), split_axis=0, concat_axis=0, tiled=True)
    own_shard = lax.dynamic_index_in_dim(shard_table, my_sequence, 0, keepdims=False)
    own_rank = lax.dynamic_index_in_dim(rank_table, my_sequence, 0, keepdims=False)
    slot_index = own_shard * capacity + own_rank
    wanted = jnp.take(arrived, slot_index, axis=0, mode="clip")
    wanted, q_first, kv_first, out_first, out_second = lax.optimization_barrier(
        (wanted, q_hops[0], kv_hops[0], *out_near)
    )
    out_pair = jnp.stack([out_first, out_second])
    q_hops.append(hop(q_first))
    kv_hops.append(hop(kv_first))
    out_third = hop(out_first, 2)
    out_fourth = move(out_second, [(1, z, 1, z - 2) for z in range(Z)])
    near_up = shift(out_pair, "y", -1)
    near_down = shift(out_pair, "y", 1)
    queries = [project_queries(rows, q_first)]
    slices = lax.all_to_all(wanted, "z", split_axis=0, concat_axis=0, tiled=True)
    per_z = X * NEIGH
    own_tokens = store_tiles.shape[1]
    column = (
        slices.reshape(Z, per_z, own_tokens, ENC)
        .transpose(1, 0, 2, 3)
        .reshape(per_z, Z * own_tokens, ENC)
    )
    q_second, kv_second = q_hops[1], kv_hops[1]
    q_hops.append(hop(q_second))
    kv_hops.append(hop(kv_second))
    out_last = jnp.where(lax.axis_index("c") == 0, out_own, out_fourth)
    far_pair = jnp.stack([out_third, out_last])
    far_up = shift(far_pair, "y", -1)
    far_down = shift(far_pair, "y", 1)
    near0 = shift(near_up[0], "y", -1)
    near1 = shift(near_down[1], "y", 1)
    queries.append(project_queries(rows, q_second))
    q_third, kv_third = q_hops[2], kv_hops[2]
    q_last = last_hop(q_weight, q_third)
    kv_last = last_hop(kv_weight, kv_third)
    far0 = shift(far_up[0], "y", -1)
    far1 = shift(far_down[1], "y", 1)
    queries.append(project_queries(rows, q_third))
    place_then = tie(place, q_last, kv_last, *queries)
    queries.append(project_queries(rows, q_last))
    kv_pieces = [kv_first, kv_second, kv_third, kv_last]
    wo = unpack(
        place_then,
        (out_pair, near_up, near0, near1, near_down, far_pair, far_up, far0, far1, far_down),
    )
    neighbours = lax.all_gather(column, ROW_AXES, axis=0, tiled=True).reshape(
        C, X, X, NEIGH, Z * own_tokens, ENC
    )

    attended = attend(tie(place, wo), queries, kv_pieces, neighbours)
    return project_and_reduce(attended, wo)


def solution(mesh):
    grid = Mesh(mesh.devices.reshape(Y, C, Z, X), ("y", "c", "z", "x"))
    tensor = ("z", "x")
    store = ("y", "c")
    in_specs = (
        P(("y", "c", "z", "x"), None),
        P(None, tensor),
        P(None, None, tensor),
        P(tensor, None),
        P(store, tensor, None),
        P(),
        P(),
    )
    out_specs = P(("y", "c", "z", "x"), None)
    return jax.shard_map(body, mesh=grid, in_specs=in_specs, out_specs=out_specs, check_vma=False)
```

```python
import functools
import math

import jax
import jax.numpy as jnp
from jax import lax
from jax.experimental import pallas as pl
from jax.experimental.pallas import tpu as pltpu
from jax.sharding import Mesh, PartitionSpec as P

HD = 128
BLOCK = 64
NTOK = 128
NEIGH = 2
Y, C, Z, X = 4, 2, 8, 4
ROW_AXES = ("c", "x")
GROUP = C * X
HEADS_HERE = 4
ENC = 896
D = 4096


def move(value, pairs):
    return lax.ppermute(value, ("c", "z"), [(c * Z + z, d * Z + w % Z) for c, z, d, w in pairs])


def hop(value, by=1):
    return move(
        value,
        [(0, z, 0, z + by) for z in range(Z)] + [(1, z, 1, z - by) for z in range(Z)],
    )


def last_hop(own, third):
    half = own.shape[0] // 2
    low = move(third[:half], [(1, z, 1, z - 1) for z in range(Z)])
    high = move(third[half:], [(0, z, 1, z + 1) for z in range(Z)])
    return jnp.where(lax.axis_index("c") == 0, own, jnp.concatenate([low, high], axis=0))


def shift(value, axis, by):
    size = lax.axis_size(axis)
    return lax.ppermute(value, axis, [(i, (i + by) % size) for i in range(size)])


def tie(value, *others):
    return lax.optimization_barrier((value, *others))[0]


IN_VMEM = pl.BlockSpec(memory_space=pltpu.VMEM)
IN_SMEM = pl.BlockSpec(memory_space=pltpu.SMEM)


OUT_COLS = D // Y
UNPACK_FLOPS = 21_000_000_000


def unpack_kernel(place, *refs):
    *pieces, wo = refs
    for b in range(2):
        own, up, far0, far1, down = pieces[5 * b : 5 * b + 5]
        for k in range(2):
            row = (2 * b + k) * HD
            for step, piece in enumerate((own.at[k], up.at[k], (far0, far1)[k], down.at[k])):
                quarter = lax.rem(place[2] + step, Y)
                column = pl.multiple_of(quarter * OUT_COLS, OUT_COLS)
                wo[row : row + HD, pl.ds(column, OUT_COLS)] = piece[...]


def unpack(place, pieces):
    return pl.pallas_call(
        unpack_kernel,
        in_specs=[IN_SMEM] + [IN_VMEM] * len(pieces),
        out_specs=IN_VMEM,
        out_shape=jax.ShapeDtypeStruct((HEADS_HERE * HD, D), jnp.bfloat16),
        cost_estimate=pl.CostEstimate(
            flops=UNPACK_FLOPS, bytes_accessed=10_000, transcendentals=0
        ),
    )(place, *pieces)


def attend_kernel(place, q0, q1, q2, q3, kv0, kv1, kv2, kv3, nb, attended, wkv):
    for h, kv in enumerate((kv0, kv1, kv2, kv3)):
        for a in range(2):
            column = (2 * h + a) * HD
            wkv[:, column : column + HD] = kv[a]
    my_c = place[0]
    my_x = place[1]
    for j in range(GROUP):
        if j < C:
            core = lax.rem(my_c + 1 + j, C)
            block = lax.rem(my_x + 2, X)
        else:
            core = lax.rem(my_c + (1 if j < C + X - 1 else 0), C)
            block = lax.rem(my_x + 3 + (j - C) % (X - 1), X)
        tokens = nb[core, :, block].reshape(NEIGH * NTOK, ENC)
        keys_values = jnp.dot(tokens, wkv[...], preferred_element_type=jnp.float32).astype(
            jnp.bfloat16
        )
        first = pl.multiple_of((core * X + block) * BLOCK, BLOCK)
        scores = jnp.concatenate(
            [
                lax.dot_general(
                    q_h[pl.ds(first, BLOCK), :],
                    keys_values[:, 2 * h * HD : (2 * h + 1) * HD],
                    (((1,), (1,)), ((), ())),
                    preferred_element_type=jnp.float32,
                )
                for h, q_h in enumerate((q0, q1, q2, q3))
            ],
            axis=0,
        )
        expo = jnp.exp(scores)
        weights = (expo / jnp.sum(expo, axis=1, keepdims=True)).astype(jnp.bfloat16)
        for h in range(HEADS_HERE):
            attended[j * BLOCK : (j + 1) * BLOCK, h * HD : (h + 1) * HD] = jnp.dot(
                weights[h * BLOCK : (h + 1) * BLOCK],
                keys_values[:, (2 * h + 1) * HD : (2 * h + 2) * HD],
                preferred_element_type=jnp.float32,
            ).astype(jnp.bfloat16)


def attend(place, queries, kvs, neighbours):
    return pl.pallas_call(
        attend_kernel,
        in_specs=[IN_SMEM] + [IN_VMEM] * (2 * HEADS_HERE + 1),
        out_specs=IN_VMEM,
        out_shape=jax.ShapeDtypeStruct((GROUP * BLOCK, HEADS_HERE * HD), jnp.bfloat16),
        scratch_shapes=[pltpu.VMEM((ENC, 2 * HEADS_HERE * HD), jnp.bfloat16)],
        compiler_params=pltpu.CompilerParams(vmem_limit_bytes=24 << 20),
        cost_estimate=pl.CostEstimate(
            flops=1_000_000, bytes_accessed=10_000, transcendentals=0
        ),
    )(place, *queries, *kvs, neighbours)


def add(*terms):
    return sum(t.astype(jnp.float32) for t in terms).astype(jnp.bfloat16)


def project_and_reduce(attended, wo):
    half = D // 2
    far_end = C * BLOCK
    other_end = far_end + (X - 1) * BLOCK

    def project(first, last):
        rows = jnp.dot(attended[first:last], wo, preferred_element_type=jnp.float32)
        return rows.astype(jnp.bfloat16).reshape(-1, BLOCK, D)

    far = project(0, far_end)
    far_swapped = shift(far[0], "c", 1)
    for_other = project(far_end, other_end)
    swapped = shift(for_other, "c", 1)
    far_sum = add(far[1], far_swapped)
    far_up = shift(far_sum[:, :half], "x", 1)
    far_down = shift(far_sum[:, half:], "x", -1)
    own = project(other_end, GROUP * BLOCK)
    empty = jnp.zeros((BLOCK, half), jnp.bfloat16)
    up_sum = add(own[2], swapped[2], jnp.concatenate([far_up, empty], axis=1))
    down_sum = add(own[0], swapped[0], jnp.concatenate([empty, far_down], axis=1))
    from_below = shift(up_sum, "x", 1)
    from_above = shift(down_sum, "x", -1)
    return add(own[1], swapped[1], from_below, from_above)


def project_queries(rows, weight):
    q_factor = 1.0 / math.sqrt(HD)
    wide = jnp.dot(rows, weight, preferred_element_type=jnp.float32)
    return (wide * q_factor).astype(jnp.bfloat16)


def body(
    decoder_rows, q_weight, kv_weight, out_weight, store_tiles, neighbour_shard, neighbour_tile
):
    store_count = Y * C
    my_sequence = lax.axis_index(("y", "c"))
    request_count = Z * X * NEIGH
    capacity = 3 * request_count // (2 * store_count)

    rows_wide = decoder_rows.astype(jnp.float32)
    normed = (
        rows_wide * lax.rsqrt(jnp.mean(rows_wide * rows_wide, axis=1, keepdims=True) + 1e-05)
    ).astype(jnp.bfloat16)
    rows = lax.all_gather(normed, ROW_AXES, axis=0, tiled=True)

    place = jnp.stack([lax.axis_index(axis) for axis in ("c", "x", "y")]).astype(jnp.int32)
    q_hops = [hop(q_weight)]
    kv_hops = [hop(kv_weight)]
    out_own = lax.dynamic_slice_in_dim(out_weight, place[2] * OUT_COLS, OUT_COLS, axis=1)
    out_near = [hop(out_own), hop(out_own, 2)]

    shard_table = neighbour_shard.reshape(store_count, request_count)
    tile_table = neighbour_tile.reshape(store_count, request_count)
    positions = jnp.arange(request_count, dtype=jnp.int32)
    before_mask = positions[None, :] < positions[:, None]
    same_shard = shard_table[:, :, None] == shard_table[:, None, :]
    rank_table = jnp.sum((same_shard & before_mask[None]).astype(jnp.int32), axis=2)
    served_here = shard_table == my_sequence
    slot_ids = jnp.arange(capacity, dtype=jnp.int32)
    slot_match = (
        served_here[:, :, None] & (rank_table[:, :, None] == slot_ids[None, None, :])
    ).astype(jnp.int32)
    slot_tile = jnp.sum(slot_match * tile_table[:, :, None], axis=1)
    outgoing = jnp.take(store_tiles, slot_tile.reshape(-1), axis=0, mode="clip")
    arrived = lax.all_to_all(outgoing, ("y", "c"), split_axis=0, concat_axis=0, tiled=True)
    own_shard = lax.dynamic_index_in_dim(shard_table, my_sequence, 0, keepdims=False)
    own_rank = lax.dynamic_index_in_dim(rank_table, my_sequence, 0, keepdims=False)
    slot_index = own_shard * capacity + own_rank
    wanted = jnp.take(arrived, slot_index, axis=0, mode="clip")
    wanted, q_first, kv_first, out_first, out_second = lax.optimization_barrier(
        (wanted, q_hops[0], kv_hops[0], *out_near)
    )
    out_pair = jnp.stack([out_first, out_second])
    q_hops.append(hop(q_first))
    kv_hops.append(hop(kv_first))
    out_third = hop(out_first, 2)
    out_fourth = move(out_second, [(1, z, 1, z - 2) for z in range(Z)])
    near_up = shift(out_pair, "y", -1)
    near_down = shift(out_pair, "y", 1)
    queries = [project_queries(rows, q_first)]
    slices = lax.all_to_all(wanted, "z", split_axis=0, concat_axis=0, tiled=True)
    per_z = X * NEIGH
    own_tokens = store_tiles.shape[1]
    column = (
        slices.reshape(Z, per_z, own_tokens, ENC)
        .transpose(1, 0, 2, 3)
        .reshape(per_z, Z * own_tokens, ENC)
    )
    q_second, kv_second = q_hops[1], kv_hops[1]
    q_hops.append(hop(q_second))
    kv_hops.append(hop(kv_second))
    out_last = jnp.where(lax.axis_index("c") == 0, out_own, out_fourth)
    far_pair = jnp.stack([out_third, out_last])
    far_up = shift(far_pair, "y", -1)
    far_down = shift(far_pair, "y", 1)
    queries.append(project_queries(rows, q_second))
    near0 = shift(near_up[0], "y", -1)
    near1 = shift(near_down[1], "y", 1)
    q_third, kv_third = q_hops[2], kv_hops[2]
    q_last = last_hop(q_weight, tie(q_third, *queries))
    kv_last = last_hop(kv_weight, kv_third)
    far0 = shift(far_up[0], "y", -1)
    far1 = shift(far_down[1], "y", 1)
    queries.append(project_queries(rows, q_third))
    place_then = tie(place, q_last, kv_last, *queries)
    kv_pieces = [kv_first, kv_second, kv_third, kv_last]
    wo = unpack(
        place_then,
        (out_pair, near_up, near0, near1, near_down, far_pair, far_up, far0, far1, far_down),
    )
    neighbours = lax.all_gather(column, ROW_AXES, axis=0, tiled=True).reshape(
        C, X, X, NEIGH, Z * own_tokens, ENC
    )

    queries.append(project_queries(rows, tie(q_last, neighbours)))
    attended = attend(tie(place, wo), queries, kv_pieces, neighbours)
    return project_and_reduce(attended, wo)


def solution(mesh):
    grid = Mesh(mesh.devices.reshape(Y, C, Z, X), ("y", "c", "z", "x"))
    tensor = ("z", "x")
    store = ("y", "c")
    in_specs = (
        P(("y", "c", "z", "x"), None),
        P(None, tensor),
        P(None, None, tensor),
        P(tensor, None),
        P(store, tensor, None),
        P(),
        P(),
    )
    out_specs = P(("y", "c", "z", "x"), None)
    return jax.shard_map(body, mesh=grid, in_specs=in_specs, out_specs=out_specs, check_vma=False)
```

```python
import functools
import math

import jax
import jax.numpy as jnp
from jax import lax
from jax.experimental import pallas as pl
from jax.experimental.pallas import tpu as pltpu
from jax.sharding import Mesh, PartitionSpec as P

HD = 128
BLOCK = 64
NTOK = 128
NEIGH = 2
Y, C, Z, X = 4, 2, 8, 4
ROW_AXES = ("c", "x")
GROUP = C * X
HEADS_HERE = 4
ENC = 896
D = 4096


def move(value, pairs):
    return lax.ppermute(value, ("c", "z"), [(c * Z + z, d * Z + w % Z) for c, z, d, w in pairs])


def hop(value, by=1):
    return move(
        value,
        [(0, z, 0, z + by) for z in range(Z)] + [(1, z, 1, z - by) for z in range(Z)],
    )


def last_hop(own, third):
    half = own.shape[0] // 2
    low = move(third[:half], [(1, z, 1, z - 1) for z in range(Z)])
    high = move(third[half:], [(0, z, 1, z + 1) for z in range(Z)])
    return jnp.where(lax.axis_index("c") == 0, own, jnp.concatenate([low, high], axis=0))


def shift(value, axis, by):
    size = lax.axis_size(axis)
    return lax.ppermute(value, axis, [(i, (i + by) % size) for i in range(size)])


def tie(value, *others):
    return lax.optimization_barrier((value, *others))[0]


IN_VMEM = pl.BlockSpec(memory_space=pltpu.VMEM)
IN_SMEM = pl.BlockSpec(memory_space=pltpu.SMEM)


OUT_COLS = D // Y
UNPACK_FLOPS = 24_000_000_000


def unpack_kernel(place, *refs):
    *pieces, wo = refs
    for b in range(2):
        own, up, far0, far1, down = pieces[5 * b : 5 * b + 5]
        for k in range(2):
            row = (2 * b + k) * HD
            for step, piece in enumerate((own.at[k], up.at[k], (far0, far1)[k], down.at[k])):
                quarter = lax.rem(place[2] + step, Y)
                column = pl.multiple_of(quarter * OUT_COLS, OUT_COLS)
                wo[row : row + HD, pl.ds(column, OUT_COLS)] = piece[...]


def unpack(place, pieces):
    return pl.pallas_call(
        unpack_kernel,
        in_specs=[IN_SMEM] + [IN_VMEM] * len(pieces),
        out_specs=IN_VMEM,
        out_shape=jax.ShapeDtypeStruct((HEADS_HERE * HD, D), jnp.bfloat16),
        compiler_params=pltpu.CompilerParams(vmem_limit_bytes=12 << 20),
        cost_estimate=pl.CostEstimate(
            flops=UNPACK_FLOPS, bytes_accessed=10_000, transcendentals=0
        ),
    )(place, *pieces)


def attend_kernel(place, q0, q1, q2, q3, kv0, kv1, kv2, kv3, nb, attended, wkv):
    for h, kv in enumerate((kv0, kv1, kv2, kv3)):
        for a in range(2):
            column = (2 * h + a) * HD
            wkv[:, column : column + HD] = kv[a]
    my_c = place[0]
    my_x = place[1]
    for j in range(GROUP):
        if j < C:
            core = lax.rem(my_c + 1 + j, C)
            block = lax.rem(my_x + 2, X)
        else:
            core = lax.rem(my_c + (1 if j < C + X - 1 else 0), C)
            block = lax.rem(my_x + 3 + (j - C) % (X - 1), X)
        tokens = nb[core, :, block].reshape(NEIGH * NTOK, ENC)
        keys_values = jnp.dot(tokens, wkv[...], preferred_element_type=jnp.float32).astype(
            jnp.bfloat16
        )
        first = pl.multiple_of((core * X + block) * BLOCK, BLOCK)
        scores = jnp.concatenate(
            [
                lax.dot_general(
                    q_h[pl.ds(first, BLOCK), :],
                    keys_values[:, 2 * h * HD : (2 * h + 1) * HD],
                    (((1,), (1,)), ((), ())),
                    preferred_element_type=jnp.float32,
                )
                for h, q_h in enumerate((q0, q1, q2, q3))
            ],
            axis=0,
        )
        expo = jnp.exp(scores)
        weights = (expo / jnp.sum(expo, axis=1, keepdims=True)).astype(jnp.bfloat16)
        for h in range(HEADS_HERE):
            attended[j * BLOCK : (j + 1) * BLOCK, h * HD : (h + 1) * HD] = jnp.dot(
                weights[h * BLOCK : (h + 1) * BLOCK],
                keys_values[:, (2 * h + 1) * HD : (2 * h + 2) * HD],
                preferred_element_type=jnp.float32,
            ).astype(jnp.bfloat16)


def attend(place, queries, kvs, neighbours):
    return pl.pallas_call(
        attend_kernel,
        in_specs=[IN_SMEM] + [IN_VMEM] * (2 * HEADS_HERE + 1),
        out_specs=IN_VMEM,
        out_shape=jax.ShapeDtypeStruct((GROUP * BLOCK, HEADS_HERE * HD), jnp.bfloat16),
        scratch_shapes=[pltpu.VMEM((ENC, 2 * HEADS_HERE * HD), jnp.bfloat16)],
        compiler_params=pltpu.CompilerParams(vmem_limit_bytes=12 << 20),
        cost_estimate=pl.CostEstimate(
            flops=1_000_000, bytes_accessed=10_000, transcendentals=0
        ),
    )(place, *queries, *kvs, neighbours)


def add(*terms):
    return sum(t.astype(jnp.float32) for t in terms).astype(jnp.bfloat16)


def project_and_reduce(attended, wo):
    half = D // 2
    far_end = C * BLOCK
    other_end = far_end + (X - 1) * BLOCK

    def project(first, last):
        rows = jnp.dot(attended[first:last], wo, preferred_element_type=jnp.float32)
        return rows.astype(jnp.bfloat16).reshape(-1, BLOCK, D)

    far = project(0, far_end)
    far_swapped = shift(far[0], "c", 1)
    for_other = project(far_end, other_end)
    swapped = shift(for_other, "c", 1)
    far_sum = add(far[1], far_swapped)
    far_up = shift(far_sum[:, :half], "x", 1)
    far_down = shift(far_sum[:, half:], "x", -1)
    own = project(other_end, GROUP * BLOCK)
    empty = jnp.zeros((BLOCK, half), jnp.bfloat16)
    up_sum = add(own[2], swapped[2], jnp.concatenate([far_up, empty], axis=1))
    down_sum = add(own[0], swapped[0], jnp.concatenate([empty, far_down], axis=1))
    from_below = shift(up_sum, "x", 1)
    from_above = shift(down_sum, "x", -1)
    return add(own[1], swapped[1], from_below, from_above)


def project_queries(rows, weight):
    q_factor = 1.0 / math.sqrt(HD)
    wide = jnp.dot(rows, weight, preferred_element_type=jnp.float32)
    return (wide * q_factor).astype(jnp.bfloat16)


def body(
    decoder_rows, q_weight, kv_weight, out_weight, store_tiles, neighbour_shard, neighbour_tile
):
    store_count = Y * C
    my_sequence = lax.axis_index(("y", "c"))
    request_count = Z * X * NEIGH
    capacity = 3 * request_count // (2 * store_count)

    rows_wide = decoder_rows.astype(jnp.float32)
    normed = (
        rows_wide * lax.rsqrt(jnp.mean(rows_wide * rows_wide, axis=1, keepdims=True) + 1e-05)
    ).astype(jnp.bfloat16)
    rows = lax.all_gather(normed, ROW_AXES, axis=0, tiled=True)

    place = jnp.stack([lax.axis_index(axis) for axis in ("c", "x", "y")]).astype(jnp.int32)
    q_hops = [hop(q_weight)]
    kv_hops = [hop(kv_weight)]
    out_own = lax.dynamic_slice_in_dim(out_weight, place[2] * OUT_COLS, OUT_COLS, axis=1)
    out_near = [hop(out_own), hop(out_own, 2)]

    shard_table = neighbour_shard.reshape(store_count, request_count)
    tile_table = neighbour_tile.reshape(store_count, request_count)
    positions = jnp.arange(request_count, dtype=jnp.int32)
    before_mask = positions[None, :] < positions[:, None]
    same_shard = shard_table[:, :, None] == shard_table[:, None, :]
    rank_table = jnp.sum((same_shard & before_mask[None]).astype(jnp.int32), axis=2)
    served_here = shard_table == my_sequence
    slot_ids = jnp.arange(capacity, dtype=jnp.int32)
    slot_match = (
        served_here[:, :, None] & (rank_table[:, :, None] == slot_ids[None, None, :])
    ).astype(jnp.int32)
    slot_tile = jnp.sum(slot_match * tile_table[:, :, None], axis=1)
    outgoing = jnp.take(store_tiles, slot_tile.reshape(-1), axis=0, mode="clip")
    arrived = lax.all_to_all(outgoing, ("y", "c"), split_axis=0, concat_axis=0, tiled=True)
    own_shard = lax.dynamic_index_in_dim(shard_table, my_sequence, 0, keepdims=False)
    own_rank = lax.dynamic_index_in_dim(rank_table, my_sequence, 0, keepdims=False)
    slot_index = own_shard * capacity + own_rank
    wanted = jnp.take(arrived, slot_index, axis=0, mode="clip")
    wanted, q_first, kv_first, out_first, out_second = lax.optimization_barrier(
        (wanted, q_hops[0], kv_hops[0], *out_near)
    )
    out_pair = jnp.stack([out_first, out_second])
    q_hops.append(hop(q_first))
    kv_hops.append(hop(kv_first))
    out_third = hop(out_first, 2)
    out_fourth = move(out_second, [(1, z, 1, z - 2) for z in range(Z)])
    near_up = shift(out_pair, "y", -1)
    near_down = shift(out_pair, "y", 1)
    queries = [project_queries(rows, q_first)]
    slices = lax.all_to_all(wanted, "z", split_axis=0, concat_axis=0, tiled=True)
    per_z = X * NEIGH
    own_tokens = store_tiles.shape[1]
    column = (
        slices.reshape(Z, per_z, own_tokens, ENC)
        .transpose(1, 0, 2, 3)
        .reshape(per_z, Z * own_tokens, ENC)
    )
    q_second, kv_second = q_hops[1], kv_hops[1]
    q_hops.append(hop(q_second))
    kv_hops.append(hop(kv_second))
    out_last = jnp.where(lax.axis_index("c") == 0, out_own, out_fourth)
    far_pair = jnp.stack([out_third, out_last])
    far_up = shift(far_pair, "y", -1)
    far_down = shift(far_pair, "y", 1)
    queries.append(project_queries(rows, q_second))
    near0 = shift(near_up[0], "y", -1)
    near1 = shift(near_down[1], "y", 1)
    q_third, kv_third = q_hops[2], kv_hops[2]
    q_last = last_hop(q_weight, tie(q_third, *queries))
    kv_last = last_hop(kv_weight, kv_third)
    far0 = shift(far_up[0], "y", -1)
    far1 = shift(far_down[1], "y", 1)
    queries.append(project_queries(rows, q_third))
    place_then = tie(place, q_last, kv_last, *queries)
    kv_pieces = [kv_first, kv_second, kv_third, kv_last]
    wo = unpack(
        place_then,
        (out_pair, near_up, near0, near1, near_down, far_pair, far_up, far0, far1, far_down),
    )
    neighbours = lax.all_gather(column, ROW_AXES, axis=0, tiled=True).reshape(
        C, X, X, NEIGH, Z * own_tokens, ENC
    )

    queries.append(project_queries(rows, tie(q_last, neighbours)))
    attended = attend(tie(place, wo), queries, kv_pieces, neighbours)
    return project_and_reduce(attended, wo)


def solution(mesh):
    grid = Mesh(mesh.devices.reshape(Y, C, Z, X), ("y", "c", "z", "x"))
    tensor = ("z", "x")
    store = ("y", "c")
    in_specs = (
        P(("y", "c", "z", "x"), None),
        P(None, tensor),
        P(None, None, tensor),
        P(tensor, None),
        P(store, tensor, None),
        P(),
        P(),
    )
    out_specs = P(("y", "c", "z", "x"), None)
    return jax.shard_map(body, mesh=grid, in_specs=in_specs, out_specs=out_specs, check_vma=False)
```
